128 devices in a mesh: dp: 16 (over y, x), tensor: 8 (over z, core).
Axes of the slice: x: 4, y: 4, z: 4, core: 2. Of those that a mesh axis runs over, the one named last changes fastest.
Arguments:
- tokens: bfloat16 [8192, 8192], P('dp', 'tensor'), may hold values from -64 to 64
- query_weight: bfloat16 [8192, 4096], P(None, 'tensor'), may hold values from -0.0625 to 0.0625
- key_value_weight: bfloat16 [2, 8192, 1024], P(None, None, 'tensor'), may hold values from -0.0625 to 0.0625
- adapter_down_weight: bfloat16 [512, 64, 8192], P('dp', None, 'tensor'), may hold values from -0.0625 to 0.0625
- adapter_up_weight: bfloat16 [512, 64, 4096], P('dp', None, 'tensor'), may hold values from -0.25 to 0.25
- response_rubrics: int32 [32, 8], P('dp'), may hold values from 0 to 511, as said below
- lengths: int32 [32], replicated, may hold values from 1 to 256, 6144 in all
- partner_attend_mask: int32 [32], P('dp'), may hold values 0 or 1
- partner_xor_mask: int32 [2], replicated, may hold values from 1 to 15
Outputs:
- attended: bfloat16 [8192, 4096], P('dp', 'tensor')
The draws below stay inside these ranges and needn't reach their ends.
Inputs may be any that keep to these rules, and one draw needn't show every extreme that they name: `response_rubrics`: each response lists 8 different adapters; among the adapters listed by the 2 responses of one index of dp, at most 2 lie in one block of 32 consecutive adapters, and some block holds exactly 2. `lengths`: some response uses all 256 positions.
All inputs are finite; a program needn't handle non-finite values. No bound on the sum of `partner_attend_mask` on one device may be relied on, other than what follows from the above.
Results may differ from the reference program's by a relative error of at most 0.012.
The reference program's roundings to bfloat16 on the way (of `rank_acts`, `queries` and `weights`) count: a program that leaves them out, or rounds other values in their place, can miss the bound.
Values may be sent and summed in bfloat16 or wider, within the bound.
No kernel may reach another device: no remote copies, remote signals or barrier semaphores. Data moves between devices by JAX's collectives and lax.ppermute only.
A program may use at most 128 MiB of HBM per device.

```python
import math
import jax
import jax.numpy as jnp
import numpy as np
from jax import lax

MODEL_WIDTH = 8192
KVH = 8
HEAD_SIZE = 128
QUERY_HEADS = 32
ADAPTER_RANK = 64
RUBRIC_COUNT = 8
MOST_PER_INDEX = 2
ADP_DEV = 32
RESP_DEV = 2
RESP = 256
ADAPTER_TOTAL = 512
RESPONSES = 32
TOKENS = 8192


def draw_tokens(key, part):
    noise = jnp.clip(jax.random.normal(jax.random.fold_in(key, 11), (TOKENS, MODEL_WIDTH), jnp.float32), -6.0, 6.0)
    result = noise
    return result.astype(jnp.bfloat16)


def draw_response_rubrics(key, part):
    owners_count = ADAPTER_TOTAL // ADP_DEV
    slot_count = RESP_DEV * RUBRIC_COUNT

    def one_device(device_key):
        first_key, second_key, third_key, fourth_key = jax.random.split(device_key, 4)
        order = jax.random.permutation(first_key, owners_count)
        tickets = jnp.repeat(order[1:], MOST_PER_INDEX)
        tickets = jax.random.permutation(second_key, tickets)[:slot_count - MOST_PER_INDEX]
        owner_ids = jnp.concatenate([jnp.full((MOST_PER_INDEX,), order[0], dtype=order.dtype), tickets]).astype(jnp.int32)
        same_owner = owner_ids[:, None] == owner_ids[None, :]
        earlier = jnp.arange(slot_count)[:, None] > jnp.arange(slot_count)[None, :]
        owner_rank = jnp.sum(jnp.where(same_owner & earlier, 1, 0), axis=1).astype(jnp.int32)
        local_table = jax.vmap(lambda table_key: jax.random.permutation(table_key, ADP_DEV))(jax.random.split(third_key, owners_count))
        local_ids = local_table[owner_ids, owner_rank].astype(jnp.int32)
        adapter_index = owner_ids * ADP_DEV + local_ids
        adapter_index = jax.random.permutation(fourth_key, adapter_index)
        return adapter_index.reshape(RESP_DEV, RUBRIC_COUNT).astype(jnp.int32)
    device_keys = jax.random.split(jax.random.fold_in(key, 21), owners_count)
    return jax.vmap(one_device)(device_keys).reshape(RESPONSES, RUBRIC_COUNT).astype(jnp.int32)


def with_ends(entries, key, smallest, top_value):
    longest = entries.shape.index(max(entries.shape))
    spots = []
    for shift in (0, 1):
        where = [jax.random.randint(jax.random.fold_in(key, axis), (), 0, length) for axis, length in enumerate(entries.shape)]
        where[longest] = (where[longest] + shift) % entries.shape[longest]
        spots.append(tuple(where))
    return entries.at[spots[0]].set(smallest).at[spots[1]].set(top_value)


def level_of(rng, dims, cuts, least, top_value):
    def one(axis_at, blocks):
        draws = jax.random.uniform(jax.random.fold_in(jax.random.fold_in(rng, 6), axis_at), (blocks,), jnp.float32, least / len(cuts), top_value / len(cuts))
        return jnp.repeat(jnp.exp(draws), dims[axis_at] // blocks).reshape((-1,) + (1,) * (len(dims) - axis_at - 1))

    loudness = one(*cuts[0])
    for cut in cuts[1:]:
        loudness = loudness * one(*cut)
    return loudness


def length_profile(amount, total, bound, lean):
    loads = [(1 << 20) // math.isqrt(rank ** lean) + 1 for rank in range(2, amount + 1)]
    spare, given = total - bound - (amount - 1), [1] * (amount - 1)
    while spare > 0:
        candidates = [i for i in range(amount - 1) if given[i] < bound]
        pool, remaining = sum([loads[i] for i in candidates]), spare
        for i in candidates:
            addition = min(bound - given[i], max(1, remaining * loads[i] // pool), spare)
            given[i] = given[i] + addition
            spare = spare - addition
    return np.array([bound] + given)


def uneven_parts(own_key, count, total, bound, lean):
    if count == 2:
        one = jax.random.randint(own_key, (), max(1, total - bound), min(bound, total - 1) + 1)
        return jnp.stack([one, total - one])
    tallies = jnp.asarray(length_profile(count, total, bound, lean), jnp.int32)
    twos = (count - 1) // 2
    source_of, taker = tallies[1:1 + 2 * twos:2], tallies[2:2 + 2 * twos:2]
    margin = jnp.minimum(source_of - 1, bound - taker)
    shifted = jax.random.randint(jax.random.fold_in(own_key, 1), (twos,), 0, 1 << 20) % (margin + 1)
    tallies = tallies.at[1:1 + 2 * twos:2].set(source_of - shifted).at[2:2 + 2 * twos:2].set(taker + shifted)
    return tallies[jax.random.permutation(jax.random.fold_in(own_key, 2), count)]


def centred(rng, dims, deviation, limit, cuts=(), kind=jnp.bfloat16):
    drawn = jax.random.normal(rng, dims, jnp.float32) * deviation
    if len(cuts) > 0:
        drawn = level_of(rng, dims, cuts, -0.22, 0.18) * drawn
    return jnp.clip(drawn, min=-limit, max=limit).astype(kind)


def setup_inputs(seed: int = 0) -> dict:
    splits = jax.random.split(jax.random.key(seed), 10)
    tokens = draw_tokens(jax.random.fold_in(splits[9], 71), 0)
    query_weight = centred(splits[1], (MODEL_WIDTH, QUERY_HEADS * HEAD_SIZE), MODEL_WIDTH ** -0.5, 0.0625, ((1, 8),))
    key_value_weight = centred(splits[2], (2, MODEL_WIDTH, KVH * HEAD_SIZE), MODEL_WIDTH ** -0.5, 0.0625, ((2, 8),))
    adapter_down_weight = centred(splits[3], (ADAPTER_TOTAL, ADAPTER_RANK, MODEL_WIDTH), MODEL_WIDTH ** -0.5, 0.0625, ((0, 16), (2, 8)))
    adapter_up_weight = centred(splits[4], (ADAPTER_TOTAL, ADAPTER_RANK, QUERY_HEADS * HEAD_SIZE), (ADAPTER_RANK * RUBRIC_COUNT) ** -0.5, 0.25, ((0, 16), (2, 8)))
    response_rubrics = draw_response_rubrics(jax.random.fold_in(splits[9], 71), 0)
    lengths = uneven_parts(splits[6], RESPONSES, RESPONSES * RESP * 3 // 4, RESP, 2).astype(jnp.int32)
    partner_attend_mask = with_ends((jax.random.randint(splits[7], (RESPONSES,), 0, 4) < 3).astype(jnp.int32), jax.random.fold_in(splits[7], 1), 0, 1)
    partner_xor_mask = jax.random.randint(splits[8], (RESP_DEV,), 1, RESPONSES // RESP_DEV).astype(jnp.int32)
    return dict(tokens=tokens, query_weight=query_weight, key_value_weight=key_value_weight, adapter_down_weight=adapter_down_weight, adapter_up_weight=adapter_up_weight, response_rubrics=response_rubrics, lengths=lengths, partner_attend_mask=partner_attend_mask, partner_xor_mask=partner_xor_mask)


def reference(tokens, query_weight, key_value_weight, adapter_down_weight, adapter_up_weight, response_rubrics, lengths, partner_attend_mask, partner_xor_mask):
    query_base = jnp.dot(tokens, query_weight, preferred_element_type=jnp.float32)
    keys = jnp.dot(tokens, key_value_weight[0], preferred_element_type=jnp.float32).astype(jnp.bfloat16)
    values = jnp.dot(tokens, key_value_weight[1], preferred_element_type=jnp.float32).astype(jnp.bfloat16)
    rows_by_resp = tokens.reshape(RESPONSES, RESP, MODEL_WIDTH)

    def low_rank(inputs):
        token_rows, adapter_index = inputs
        down_weight_rows = jnp.take(adapter_down_weight, adapter_index, axis=0).reshape(RUBRIC_COUNT * ADAPTER_RANK, MODEL_WIDTH)
        up_weight_rows = jnp.take(adapter_up_weight, adapter_index, axis=0).reshape(RUBRIC_COUNT * ADAPTER_RANK, QUERY_HEADS * HEAD_SIZE)
        rank_acts = lax.dot_general(token_rows, down_weight_rows, (((1,), (1,)), ((), ())), preferred_element_type=jnp.float32).astype(jnp.bfloat16)
        return jnp.dot(rank_acts, up_weight_rows, preferred_element_type=jnp.float32)
    delta = lax.map(low_rank, (rows_by_resp, response_rubrics)).reshape(TOKENS, QUERY_HEADS * HEAD_SIZE)
    queries = (query_base + delta).astype(jnp.bfloat16)
    per_group = QUERY_HEADS // KVH
    query_resp = queries.reshape(RESPONSES, RESP, KVH, per_group, HEAD_SIZE)
    key_resp = keys.reshape(RESPONSES, RESP, KVH, HEAD_SIZE)
    value_resp = values.reshape(RESPONSES, RESP, KVH, HEAD_SIZE)
    positions = jnp.arange(RESP).astype(jnp.int32)
    scale = 1.0 / math.sqrt(HEAD_SIZE)

    def attend(index):
        device = index // RESP_DEV
        slot_pos = index % RESP_DEV
        mask_bits = partner_xor_mask[slot_pos]
        mate = (jnp.bitwise_xor(device, mask_bits) * RESP_DEV + slot_pos).astype(jnp.int32)
        own_len = lengths[index]
        mate_len = lengths[mate]
        key_all = jnp.concatenate([key_resp[index], key_resp[mate]], axis=0).astype(jnp.float32)
        value_all = jnp.concatenate([value_resp[index], value_resp[mate]], axis=0).astype(jnp.float32)
        scores = jnp.einsum('tkgh,ukh->kgtu', query_resp[index].astype(jnp.float32), key_all) * scale
        own_ok = (positions[None, :] <= positions[:, None]) & (positions[None, :] < own_len)
        mate_ok = (positions[None, :] < mate_len) & (partner_attend_mask[index] == 1)
        allowed = jnp.concatenate([own_ok, jnp.broadcast_to(mate_ok, (RESP, RESP))], axis=1)
        scores = jnp.where(allowed, scores, -1e+30)
        row_top = lax.optimization_barrier(jnp.max(scores, axis=-1, keepdims=True))
        raised = jnp.where(allowed, jnp.exp(scores - row_top), 0.0)
        weights = (raised / lax.optimization_barrier(jnp.sum(raised, axis=-1, keepdims=True))).astype(jnp.bfloat16)
        mixed = jnp.einsum('kgtu,ukh->tkgh', weights.astype(jnp.float32), value_all)
        return mixed.reshape(RESP, QUERY_HEADS * HEAD_SIZE).astype(jnp.bfloat16)
    attended = lax.map(attend, jnp.arange(RESPONSES).astype(jnp.int32))
    return attended.reshape(TOKENS, QUERY_HEADS * HEAD_SIZE)
```

```python
from functools import partial
import math

import jax
import jax.numpy as jnp
from jax import lax
from jax.sharding import PartitionSpec as P

HEAD_SIZE = 128
MOST_PER_INDEX = 2


def slot_layout(adapter_index, adapters_by_owner):
    owner_ids = adapter_index // adapters_by_owner
    local_ids = adapter_index % adapters_by_owner
    slot_count = adapter_index.shape[-1]
    same_owner = owner_ids[..., :, None] == owner_ids[..., None, :]
    earlier = jnp.arange(slot_count)[:, None] > jnp.arange(slot_count)[None, :]
    owner_rank = jnp.sum(jnp.where(same_owner & earlier, 1, 0), axis=-1).astype(jnp.int32)
    return (owner_ids, local_ids, owner_rank)


def from_partner(block, mask):
    count = lax.axis_size("dp")
    moves = [
        partial(lax.ppermute, axis_name="dp", perm=[(source, source ^ flip) for source in range(count)])
        for flip in range(1, count)
    ]
    return lax.switch(mask - 1, moves, block)


def on_device(
    tokens,
    query_weight,
    key_value_weight,
    adapter_down_weight,
    adapter_up_weight,
    response_rubrics,
    lengths,
    partner_attend_mask,
    partner_xor_mask,
):
    owner_groups = lax.axis_size("dp")
    tensor_size = lax.axis_size("tensor")
    own_index = lax.axis_index("dp")
    resp_dev, rubrics = response_rubrics.shape
    partner_dev = jnp.bitwise_xor(own_index, partner_xor_mask)
    adapters_by_owner, rank_extent, feature_shard = adapter_down_weight.shape
    head_columns = query_weight.shape[1]
    kv_cols = key_value_weight.shape[2]
    slot_count = resp_dev * rubrics
    tok_rows = tokens.shape[0]
    resp_len = tok_rows // resp_dev
    wide = lax.all_gather(tokens, "tensor", axis=1, tiled=True)
    slot_ids = response_rubrics.reshape(slot_count)
    owner_ids, local_ids, owner_rank = slot_layout(slot_ids, adapters_by_owner)
    buffer_slot = owner_ids * MOST_PER_INDEX + owner_rank
    columns_all = jnp.arange(owner_groups * MOST_PER_INDEX, dtype=jnp.int32)
    hits = buffer_slot[:, None] == columns_all[None, :]
    wanted = jnp.sum(jnp.where(hits, local_ids[:, None], 0), axis=0).reshape(
        owner_groups, MOST_PER_INDEX
    )
    asked = lax.all_to_all(wanted, "dp", split_axis=0, concat_axis=0, tiled=True)
    asked = asked.reshape(owner_groups * MOST_PER_INDEX)
    shipped_down = jnp.take(adapter_down_weight, asked, axis=0, mode="clip").reshape(
        owner_groups, MOST_PER_INDEX, rank_extent, feature_shard
    )
    got_down = lax.all_to_all(shipped_down, "dp", split_axis=0, concat_axis=0, tiled=True)
    shipped_up = jnp.take(adapter_up_weight, asked, axis=0, mode="clip").reshape(
        owner_groups, MOST_PER_INDEX, rank_extent, head_columns
    )
    got_up = lax.all_to_all(shipped_up, "dp", split_axis=0, concat_axis=0, tiled=True)
    down_sel = jnp.take(
        got_down.reshape(owner_groups * MOST_PER_INDEX, rank_extent, feature_shard),
        buffer_slot, axis=0, mode="clip",
    ).reshape(resp_dev, rubrics * rank_extent, feature_shard)
    up_sel = jnp.take(
        got_up.reshape(owner_groups * MOST_PER_INDEX, rank_extent, head_columns),
        buffer_slot, axis=0, mode="clip",
    ).reshape(resp_dev, rubrics * rank_extent, head_columns)
    token_blocks = tokens.reshape(resp_dev, resp_len, feature_shard)
    partial_acts = jnp.einsum(
        "jtd,jrd->jtr", token_blocks, down_sel, preferred_element_type=jnp.float32
    )
    ranks = rubrics * rank_extent
    pieces = partial_acts.reshape(tensor_size, tok_rows // tensor_size, ranks)
    pieces = lax.all_to_all(pieces, "tensor", split_axis=0, concat_axis=0, tiled=True)
    summed = jnp.sum(pieces, axis=0).astype(jnp.bfloat16)
    rank_acts = lax.all_gather(summed, "tensor", axis=0, tiled=True).reshape(
        resp_dev, resp_len, ranks
    )
    keyval = jnp.einsum(
        "tw,cwk->ctk", wide, key_value_weight, preferred_element_type=jnp.float32
    ).astype(jnp.bfloat16).reshape(2, resp_dev, resp_len, kv_cols)
    mate_keyval = jnp.stack(
        [from_partner(keyval[:, j], partner_xor_mask[j]) for j in range(resp_dev)], axis=1
    )
    query_acc = jnp.dot(wide, query_weight, preferred_element_type=jnp.float32)
    delta = jnp.einsum(
        "jtr,jrq->jtq", rank_acts, up_sel, preferred_element_type=jnp.float32
    ).reshape(tok_rows, head_columns)
    queries = (query_acc + delta).astype(jnp.bfloat16)
    heads_dev = head_columns // HEAD_SIZE
    kv_heads = kv_cols // HEAD_SIZE
    per_group = heads_dev // kv_heads
    query_blocks = queries.reshape(resp_dev, resp_len, kv_heads, per_group, HEAD_SIZE)
    both = jnp.concatenate([keyval, mate_keyval], axis=2).reshape(
        2, resp_dev, 2 * resp_len, kv_heads, HEAD_SIZE
    )
    key_all, value_all = both[0], both[1]
    scale = 1.0 / math.sqrt(HEAD_SIZE)
    scores = (
        jnp.einsum("jtkgh,jukh->jkgtu", query_blocks, key_all, preferred_element_type=jnp.float32)
        * scale
    )
    own_lens = lax.dynamic_slice_in_dim(lengths, own_index * resp_dev, resp_dev)
    mate_index = partner_dev * resp_dev + jnp.arange(resp_dev, dtype=jnp.int32)
    mate_lens = jnp.take(lengths, mate_index, axis=0, mode="clip")
    positions = jnp.arange(resp_len, dtype=jnp.int32)
    own_ok = (positions[None, None, :] <= positions[None, :, None]) & (
        positions[None, None, :] < own_lens[:, None, None]
    )
    mate_ok = (positions[None, None, :] < mate_lens[:, None, None]) & (
        partner_attend_mask[:, None, None] == 1
    )
    allowed = jnp.concatenate(
        [own_ok, jnp.broadcast_to(mate_ok, (resp_dev, resp_len, resp_len))], axis=2
    )
    allowed = allowed[:, None, None, :, :]
    scores = jnp.where(allowed, scores, -1e30)
    row_top = jnp.max(scores, axis=-1, keepdims=True)
    raised = jnp.where(allowed, jnp.exp(scores - row_top), 0.0)
    weights = (raised / jnp.sum(raised, axis=-1, keepdims=True)).astype(jnp.bfloat16)
    mixed = jnp.einsum("jkgtu,jukh->jtkgh", weights, value_all, preferred_element_type=jnp.float32)
    return mixed.reshape(tok_rows, head_columns).astype(jnp.bfloat16)


def solution(mesh):
    in_specs = (
        P("dp", "tensor"),
        P(None, "tensor"),
        P(None, None, "tensor"),
        P("dp", None, "tensor"),
        P("dp", None, "tensor"),
        P("dp", None),
        P(),
        P("dp"),
        P(),
    )
    out_specs = P("dp", "tensor")
    return jax.shard_map(
        on_device, mesh=mesh, in_specs=in_specs, out_specs=out_specs, check_vma=False
    )
```

```python
from functools import partial
import math

import jax
import jax.numpy as jnp
from jax import lax
from jax.experimental import pallas as pl
from jax.experimental.pallas import tpu as pltpu
from jax.sharding import PartitionSpec as P

HEAD_SIZE = 128
MOST_PER_INDEX = 2
LANES = 128


def slot_layout(adapter_index, adapters_by_owner):
    owner_ids = adapter_index // adapters_by_owner
    local_ids = adapter_index % adapters_by_owner
    same_owner = owner_ids[:, None] == owner_ids[None, :]
    smaller = adapter_index[None, :] < adapter_index[:, None]
    owner_rank = jnp.any(same_owner & smaller, axis=1).astype(jnp.int32)
    return owner_ids, local_ids, owner_ids * MOST_PER_INDEX + owner_rank


def from_partner(block, mask):
    count = lax.axis_size("dp")
    moves = [
        partial(lax.ppermute, axis_name="dp", perm=[(source, source ^ flip) for source in range(count)])
        for flip in range(1, count)
    ]
    return lax.switch(mask - 1, moves, block)


def take_asked(table, asked):
    return jnp.take(table, asked[:, :MOST_PER_INDEX].reshape(-1), axis=0, mode="clip")


def partial_kernel(slots_ref, tokens_ref, *refs):
    downs, out_ref = refs[:-1], refs[-1]
    rows = jnp.concatenate([d[0] for d in downs], axis=0)
    out_ref[...] = lax.dot_general(
        tokens_ref[...], rows, (((1,), (1,)), ((), ())), preferred_element_type=jnp.float32
    ).astype(out_ref.dtype)


def partial_rank_acts(tokens, got_down, slots, resp_dev, rubrics):
    rows, features = tokens.shape
    ranks = got_down.shape[1]
    resp_len = rows // resp_dev

    def down_spec(s):
        return pl.BlockSpec((1, ranks, features), lambda j, slots_ref: (slots_ref[j * rubrics + s], 0, 0))

    return pl.pallas_call(
        partial_kernel,
        out_shape=jax.ShapeDtypeStruct((rows, rubrics * ranks), jnp.bfloat16),
        grid_spec=pltpu.PrefetchScalarGridSpec(
            num_scalar_prefetch=1,
            grid=(resp_dev,),
            in_specs=[pl.BlockSpec((resp_len, features), lambda j, slots_ref: (j, 0))]
            + [down_spec(s) for s in range(rubrics)],
            out_specs=pl.BlockSpec((resp_len, rubrics * ranks), lambda j, slots_ref: (j, 0)),
        ),
        compiler_params=pltpu.CompilerParams(vmem_limit_bytes=32 << 20),
        name="partial_rank_acts",
    )(slots, tokens, *([got_down] * rubrics))


def attend_kernel(
    slots_ref, lens_ref, mates_ref, partials_ref, base_ref, own_ref, mate_ref, *refs
):
    ups, out_ref = refs[:-1], refs[-1]
    j = pl.program_id(0)
    acts = jnp.sum(partials_ref[...].astype(jnp.float32), axis=0).astype(jnp.bfloat16)
    up_rows = jnp.concatenate([u[0] for u in ups], axis=0)
    delta = jnp.dot(acts, up_rows, preferred_element_type=jnp.float32)
    queries = (base_ref[...] + delta).astype(jnp.bfloat16)
    rows, columns = queries.shape
    scale = math.log2(math.e) / math.sqrt(HEAD_SIZE)
    keys = jnp.concatenate([own_ref[0], mate_ref[0]], axis=0)
    values = jnp.concatenate([own_ref[1], mate_ref[1]], axis=0)
    position = lax.broadcasted_iota(jnp.int32, (rows, 2 * rows), 0)
    key_at = lax.broadcasted_iota(jnp.int32, (rows, 2 * rows), 1)
    own_ok = (key_at <= position) & (key_at < lens_ref[j])
    mate_ok = (key_at >= rows) & (key_at < rows + mates_ref[j])
    allowed = own_ok | mate_ok
    for h in range(columns // HEAD_SIZE):
        cut = slice(h * HEAD_SIZE, (h + 1) * HEAD_SIZE)
        scores = lax.dot_general(
            queries[:, cut], keys, (((1,), (1,)), ((), ())), preferred_element_type=jnp.float32
        )
        scores = jnp.where(allowed, scores, -1e30)
        top = jnp.max(scores, axis=1, keepdims=True)
        raised = jnp.exp2((scores - top) * scale)
        weights = (raised * (1.0 / jnp.sum(raised, axis=1, keepdims=True))).astype(jnp.bfloat16)
        out_ref[:, cut] = jnp.dot(weights, values, preferred_element_type=jnp.float32).astype(
            out_ref.dtype
        )


def attend(partials, base, keyval, mate_keyval, got_up, slots, own_lens, mate_lens, rubrics):
    rows, columns = base.shape
    resp_dev = own_lens.shape[0]
    resp_len = rows // resp_dev
    shards = partials.shape[0]
    ranks = got_up.shape[1]

    def up_spec(s):
        return pl.BlockSpec((1, ranks, columns), lambda j, slots_ref, *_: (slots_ref[j * rubrics + s], 0, 0))

    kv_spec = pl.BlockSpec((2, resp_len, HEAD_SIZE), lambda j, *_: (0, j, 0))
    return pl.pallas_call(
        attend_kernel,
        out_shape=jax.ShapeDtypeStruct((rows, columns), jnp.bfloat16),
        grid_spec=pltpu.PrefetchScalarGridSpec(
            num_scalar_prefetch=3,
            grid=(resp_dev,),
            in_specs=[
                pl.BlockSpec((shards, resp_len, rubrics * ranks), lambda j, *_: (0, j, 0)),
                pl.BlockSpec((resp_len, columns), lambda j, *_: (j, 0)),
                kv_spec,
                kv_spec,
            ]
            + [up_spec(s) for s in range(rubrics)],
            out_specs=pl.BlockSpec((resp_len, columns), lambda j, *_: (j, 0)),
        ),
        compiler_params=pltpu.CompilerParams(vmem_limit_bytes=40 << 20),
        name="attend",
    )(slots, own_lens, mate_lens, pltpu.with_memory_space_constraint(partials, pltpu.HBM), pltpu.with_memory_space_constraint(base, pltpu.HBM), keyval, mate_keyval, *([got_up] * rubrics))


def on_device(
    tokens,
    query_weight,
    key_value_weight,
    adapter_down_weight,
    adapter_up_weight,
    response_rubrics,
    lengths,
    partner_attend_mask,
    partner_xor_mask,
):
    owner_groups = lax.axis_size("dp")
    own_index = lax.axis_index("dp")
    resp_dev, rubrics = response_rubrics.shape
    partner_dev = jnp.bitwise_xor(own_index, partner_xor_mask)
    adapters_by_owner, rank_extent, feature_shard = adapter_down_weight.shape
    head_columns = query_weight.shape[1]
    kv_cols = key_value_weight.shape[2]
    slot_count = resp_dev * rubrics
    tok_rows = tokens.shape[0]
    resp_len = tok_rows // resp_dev
    wide = lax.all_gather(tokens, "tensor", axis=1, tiled=True)
    slot_ids = response_rubrics.reshape(slot_count)
    owner_ids, local_ids, buffer_slot = slot_layout(slot_ids, adapters_by_owner)
    cells = lax.broadcasted_iota(jnp.int32, (owner_groups, LANES), 0) * MOST_PER_INDEX
    lane = lax.broadcasted_iota(jnp.int32, (owner_groups, LANES), 1)
    cells = jnp.where(lane < MOST_PER_INDEX, cells + lane, -1)
    wanted = jnp.max(
        jnp.where(buffer_slot[:, None, None] == cells[None], local_ids[:, None, None], 0), axis=0
    )
    asked = lax.all_to_all(wanted, "dp", split_axis=0, concat_axis=0, tiled=True)
    shipped_down = take_asked(adapter_down_weight, asked)
    shipped_down = shipped_down.reshape(owner_groups, MOST_PER_INDEX, rank_extent, feature_shard)
    got_down = lax.all_to_all(shipped_down, "dp", split_axis=0, concat_axis=0, tiled=True)
    shipped_up = take_asked(adapter_up_weight, asked)
    shipped_up = shipped_up.reshape(owner_groups, MOST_PER_INDEX, rank_extent, head_columns)
    keyval = jnp.einsum(
        "tw,cwk->ctk", wide, key_value_weight, preferred_element_type=jnp.float32
    ).astype(jnp.bfloat16)
    base = jnp.dot(wide, query_weight, preferred_element_type=jnp.float32)
    own_keyval = keyval.reshape(2, resp_dev, resp_len, kv_cols)
    own_keyval, base = lax.optimization_barrier((own_keyval, base))
    mate_first = from_partner(own_keyval[:, 0], partner_xor_mask[0])
    got_down, shipped_up, mate_first, own_keyval = lax.optimization_barrier(
        (got_down, shipped_up, mate_first, own_keyval)
    )
    got_up = lax.all_to_all(shipped_up, "dp", split_axis=0, concat_axis=0, tiled=True)
    partials = partial_rank_acts(
        tokens, got_down.reshape(-1, rank_extent, feature_shard), buffer_slot, resp_dev, rubrics
    )
    partials, own_keyval = lax.optimization_barrier((partials, own_keyval))
    partials = lax.all_gather(partials, "tensor", axis=0)
    mate_second = from_partner(own_keyval[:, 1], partner_xor_mask[1])
    mate_keyval = jnp.concatenate([mate_first, mate_second], axis=1)
    own_lens = lax.dynamic_slice_in_dim(lengths, own_index * resp_dev, resp_dev)
    mate_index = partner_dev * resp_dev + jnp.arange(resp_dev, dtype=jnp.int32)
    mate_lens = jnp.take(lengths, mate_index, axis=0, mode="clip")
    mate_lens = jnp.where(partner_attend_mask == 1, mate_lens, 0)
    return attend(
        partials, base, keyval, mate_keyval, got_up.reshape(-1, rank_extent, head_columns),
        buffer_slot, own_lens, mate_lens, rubrics,
    )


def solution(mesh):
    in_specs = (
        P("dp", "tensor"),
        P(None, "tensor"),
        P(None, None, "tensor"),
        P("dp", None, "tensor"),
        P("dp", None, "tensor"),
        P("dp", None),
        P(),
        P("dp"),
        P(),
    )
    out_specs = P("dp", "tensor")
    return jax.shard_map(
        on_device, mesh=mesh, in_specs=in_specs, out_specs=out_specs, check_vma=False
    )
```

```python
from functools import partial
import math

import jax
import jax.numpy as jnp
from jax import lax
from jax.experimental import pallas as pl
from jax.experimental.pallas import tpu as pltpu
from jax.sharding import PartitionSpec as P

HEAD_SIZE = 128
MOST_PER_INDEX = 2
LANES = 128


def slot_layout(adapter_index, adapters_by_owner):
    owner_ids = adapter_index // adapters_by_owner
    local_ids = adapter_index % adapters_by_owner
    same_owner = owner_ids[:, None] == owner_ids[None, :]
    smaller = adapter_index[None, :] < adapter_index[:, None]
    owner_rank = jnp.any(same_owner & smaller, axis=1).astype(jnp.int32)
    return owner_ids, local_ids, owner_ids * MOST_PER_INDEX + owner_rank


def from_partner(block, mask):
    count = lax.axis_size("dp")
    moves = [
        partial(lax.ppermute, axis_name="dp", perm=[(source, source ^ flip) for source in range(count)])
        for flip in range(1, count)
    ]
    return lax.switch(mask - 1, moves, block)


def take_asked(table, asked):
    return jnp.take(table, asked[:, :MOST_PER_INDEX].reshape(-1), axis=0, mode="clip")


def project_kernel(pieces, order_ref, query_weight_ref, keyval_weight_ref, *refs):
    base_ref, keyval_ref, rows_ref, query_acc, keyval_acc, sems = refs[-6:]
    step = pl.program_id(0)
    last = len(pieces) - 1

    def fetches(i):
        copies, first = [], sum(pieces[:i])
        for piece in range(pieces[i]):
            source = refs[first + piece]
            rows = pl.ds(piece * source.shape[0], source.shape[0])
            copies.append(
                pltpu.make_async_copy(source, rows_ref.at[i % 2, rows], sems.at[i % 2, piece])
            )
        return copies

    @pl.when(step == 0)
    def _():
        for copy in fetches(0):
            copy.start()
        query_acc[...] = jnp.zeros_like(query_acc)
        keyval_acc[...] = jnp.zeros_like(keyval_acc)

    for i in range(len(pieces)):

        @pl.when(step == i)
        def _(i=i):
            if i < last:
                for copy in fetches(i + 1):
                    copy.start()
            for copy in fetches(i):
                copy.wait()

    rows = rows_ref[step % 2]
    both = jnp.concatenate([keyval_weight_ref[0], keyval_weight_ref[1]], axis=1)
    query_acc[...] += jnp.dot(rows, query_weight_ref[...], preferred_element_type=jnp.float32)
    keyval_acc[...] += jnp.dot(rows, both, preferred_element_type=jnp.float32)

    @pl.when(step == last)
    def _():
        width = keyval_ref.shape[2]
        base_ref[...] = query_acc[...]
        keyval_ref[0] = keyval_acc[:, :width].astype(keyval_ref.dtype)
        keyval_ref[1] = keyval_acc[:, width:].astype(keyval_ref.dtype)


def project(blocks, order, query_weight, keyval_weight):
    rows, features = blocks[0][0].shape
    pieces = tuple(len(block) for block in blocks)
    arrays = [piece for block in blocks for piece in block]
    columns = query_weight.shape[1]
    width = keyval_weight.shape[2]
    return pl.pallas_call(
        partial(project_kernel, pieces),
        out_shape=(
            jax.ShapeDtypeStruct((rows, columns), jnp.float32),
            jax.ShapeDtypeStruct((2, rows, width), jnp.bfloat16),
        ),
        grid_spec=pltpu.PrefetchScalarGridSpec(
            num_scalar_prefetch=1,
            grid=(len(blocks),),
            in_specs=[
                pl.BlockSpec((features, columns), lambda i, order_ref: (order_ref[i], 0)),
                pl.BlockSpec((2, features, width), lambda i, order_ref: (0, order_ref[i], 0)),
            ]
            + [pl.BlockSpec(memory_space=pl.ANY)] * len(arrays),
            out_specs=(
                pl.BlockSpec((rows, columns), lambda i, *_: (0, 0)),
                pl.BlockSpec((2, rows, width), lambda i, *_: (0, 0, 0)),
            ),
            scratch_shapes=[
                pltpu.VMEM((2, rows, features), jnp.bfloat16),
                pltpu.VMEM((rows, columns), jnp.float32),
                pltpu.VMEM((rows, 2 * width), jnp.float32),
                pltpu.SemaphoreType.DMA((2, max(pieces))),
            ],
        ),
        compiler_params=pltpu.CompilerParams(vmem_limit_bytes=32 << 20),
        name="project",
    )(order, *[pltpu.with_memory_space_constraint(x, pltpu.HBM) for x in (query_weight, keyval_weight, *arrays)])


def across_tensor(block, flip):
    size = lax.axis_size("tensor")
    return lax.ppermute(block, "tensor", [(source, source ^ flip) for source in range(size)])


def along_column(block, step):
    size = lax.axis_size("tensor")
    return lax.ppermute(block, "tensor", [(source, (source + 2 * step) % size) for source in range(size)])


def neighbour_features(tokens):
    return along_column(tokens, 1), along_column(tokens, -1)


def all_features(tokens, before, after):
    size = lax.axis_size("tensor")
    own = lax.axis_index("tensor")
    half = tokens.shape[0] // 2
    opposite = (along_column(before[:half], 1), along_column(after[half:], -1))
    held = [(tokens,), (before,), (after,), opposite]
    blocks, order = [], []
    for offset, pieces in zip((0, size - 2, 2, 4), held):
        index = (own + offset) % size
        blocks += [pieces, tuple(across_tensor(piece, 1) for piece in pieces)]
        order += [index, jnp.bitwise_xor(index, 1)]
    return blocks, jnp.stack(order)


def sum_over_tensor(keep, send, beside):
    size = lax.axis_size("tensor")
    pair = keep + across_tensor(send, 1)
    small = pair.astype(jnp.bfloat16)
    others = [across_tensor(small, flip) for flip in range(2, size, 2)]
    extra = beside(small)
    *others, extra = lax.optimization_barrier((*others, extra))
    total = pair
    for other in others:
        total = total + other.astype(jnp.float32)
    acts = total.astype(jnp.bfloat16)
    return acts, across_tensor(acts, 1), extra


def sum_over_tensor_plain(keep, send, core, extra):
    both = jnp.stack([keep, send])
    both = jnp.where(core == 0, both, both[::-1])
    total = both
    for flip in range(1, lax.axis_size("tensor")):
        total = total + across_tensor(both, flip)
    total = total.astype(jnp.bfloat16)
    total = jnp.where(core == 0, total, total[::-1])
    return total[0], total[1], extra


def partial_kernel(slots_ref, core_ref, tokens_ref, *refs):
    downs, keep_ref, send_ref = refs[:-2], refs[-2], refs[-1]
    rows = jnp.concatenate([d[0] for d in downs], axis=0)
    acts = lax.dot_general(
        tokens_ref[...], rows, (((1,), (1,)), ((), ())), preferred_element_type=jnp.float32
    )
    kept = pl.program_id(0) == core_ref[0]

    @pl.when(kept)
    def _():
        keep_ref[...] = acts

    @pl.when(jnp.logical_not(kept))
    def _():
        send_ref[...] = acts


def partial_rank_acts(tokens, got_down, slots, core, rubrics):
    rows, features = tokens.shape
    ranks = got_down.shape[1]
    resp_len = rows // 2

    def down_spec(s):
        return pl.BlockSpec((1, ranks, features), lambda j, slots_ref, _: (slots_ref[j * rubrics + s], 0, 0))

    half = jax.ShapeDtypeStruct((resp_len, rubrics * ranks), jnp.float32)
    half_spec = pl.BlockSpec(half.shape, lambda j, *_: (0, 0))
    return pl.pallas_call(
        partial_kernel,
        out_shape=(half, half),
        grid_spec=pltpu.PrefetchScalarGridSpec(
            num_scalar_prefetch=2,
            grid=(2,),
            in_specs=[pl.BlockSpec((resp_len, features), lambda j, *_: (j, 0))]
            + [down_spec(s) for s in range(rubrics)],
            out_specs=(half_spec, half_spec),
        ),
        compiler_params=pltpu.CompilerParams(vmem_limit_bytes=32 << 20),
        cost_estimate=pl.CostEstimate(flops=2 * rows * features * ranks * rubrics, bytes_accessed=4 << 20, transcendentals=0),
        name="partial_rank_acts",
    )(slots, core, tokens, *([got_down] * rubrics))


def attend_kernel(
    slots_ref, lens_ref, mates_ref, core_ref, same_ref, other_ref, base_ref, own_ref, mate_ref, *refs
):
    ups, out_ref = refs[:-1], refs[-1]
    j = pl.program_id(0)
    acts = jnp.where(j == core_ref[0], same_ref[...], other_ref[...])
    up_rows = jnp.concatenate([u[0] for u in ups], axis=0)
    delta = jnp.dot(acts, up_rows, preferred_element_type=jnp.float32)
    queries = (base_ref[...] + delta).astype(jnp.bfloat16)
    rows, columns = queries.shape
    scale = math.log2(math.e) / math.sqrt(HEAD_SIZE)
    keys = jnp.concatenate([own_ref[0], mate_ref[0]], axis=0)
    values = jnp.concatenate([own_ref[1], mate_ref[1]], axis=0)
    position = lax.broadcasted_iota(jnp.int32, (rows, 2 * rows), 0)
    key_at = lax.broadcasted_iota(jnp.int32, (rows, 2 * rows), 1)
    own_ok = (key_at <= position) & (key_at < lens_ref[j])
    mate_ok = (key_at >= rows) & (key_at < rows + mates_ref[j])
    allowed = own_ok | mate_ok
    for h in range(columns // HEAD_SIZE):
        cut = slice(h * HEAD_SIZE, (h + 1) * HEAD_SIZE)
        scores = lax.dot_general(
            queries[:, cut], keys, (((1,), (1,)), ((), ())), preferred_element_type=jnp.float32
        )
        scores = jnp.where(allowed, scores, -1e30)
        top = jnp.max(scores, axis=1, keepdims=True)
        raised = jnp.exp2((scores - top) * scale)
        weights = (raised * (1.0 / jnp.sum(raised, axis=1, keepdims=True))).astype(jnp.bfloat16)
        out_ref[:, cut] = jnp.dot(weights, values, preferred_element_type=jnp.float32).astype(
            out_ref.dtype
        )


def attend(acts, base, keyval, mate_keyvals, got_up, slots, own_lens, mate_lens, core, rubrics):
    rows, columns = base.shape
    resp_dev = own_lens.shape[0]
    resp_len = rows // resp_dev
    ranks = got_up.shape[1]

    def up_spec(s):
        return pl.BlockSpec((1, ranks, columns), lambda j, slots_ref, *_: (slots_ref[j * rubrics + s], 0, 0))

    acts_spec = pl.BlockSpec(acts[0].shape, lambda j, *_: (0, 0))
    kv_spec = pl.BlockSpec((2, resp_len, HEAD_SIZE), lambda j, *_: (0, j, 0))
    return pl.pallas_call(
        attend_kernel,
        out_shape=jax.ShapeDtypeStruct((rows, columns), jnp.bfloat16),
        grid_spec=pltpu.PrefetchScalarGridSpec(
            num_scalar_prefetch=4,
            grid=(resp_dev,),
            in_specs=[
                acts_spec,
                acts_spec,
                pl.BlockSpec((resp_len, columns), lambda j, *_: (j, 0)),
                kv_spec,
                kv_spec,
            ]
            + [up_spec(s) for s in range(rubrics)],
            out_specs=pl.BlockSpec((resp_len, columns), lambda j, *_: (j, 0)),
        ),
        compiler_params=pltpu.CompilerParams(vmem_limit_bytes=40 << 20),
        name="attend",
    )(slots, own_lens, mate_lens, core, *acts, pltpu.with_memory_space_constraint(base, pltpu.HBM), keyval, mate_keyvals, *([got_up] * rubrics))


def on_device(
    tokens,
    query_weight,
    key_value_weight,
    adapter_down_weight,
    adapter_up_weight,
    response_rubrics,
    lengths,
    partner_attend_mask,
    partner_xor_mask,
):
    owner_groups = lax.axis_size("dp")
    own_index = lax.axis_index("dp")
    resp_dev, rubrics = response_rubrics.shape
    partner_dev = jnp.bitwise_xor(own_index, partner_xor_mask)
    adapters_by_owner, rank_extent, feature_shard = adapter_down_weight.shape
    head_columns = query_weight.shape[1]
    kv_cols = key_value_weight.shape[2]
    slot_count = resp_dev * rubrics
    tok_rows = tokens.shape[0]
    resp_len = tok_rows // resp_dev
    before, after = neighbour_features(tokens)
    slot_ids = response_rubrics.reshape(slot_count)
    owner_ids, local_ids, buffer_slot = slot_layout(slot_ids, adapters_by_owner)
    cells = lax.broadcasted_iota(jnp.int32, (owner_groups, LANES), 0) * MOST_PER_INDEX
    lane = lax.broadcasted_iota(jnp.int32, (owner_groups, LANES), 1)
    cells = jnp.where(lane < MOST_PER_INDEX, cells + lane, -1)
    wanted = jnp.max(
        jnp.where(buffer_slot[:, None, None] == cells[None], local_ids[:, None, None], 0), axis=0
    )
    asked = lax.all_to_all(wanted, "dp", split_axis=0, concat_axis=0, tiled=True)
    shipped_down = take_asked(adapter_down_weight, asked)
    shipped_down = shipped_down.reshape(owner_groups, MOST_PER_INDEX, rank_extent, feature_shard)
    shipped_down, before, after = lax.optimization_barrier((shipped_down, before, after))
    got_down = lax.all_to_all(shipped_down, "dp", split_axis=0, concat_axis=0, tiled=True)
    shipped_up = take_asked(adapter_up_weight, asked)
    shipped_up = shipped_up.reshape(owner_groups, MOST_PER_INDEX, rank_extent, head_columns)
    blocks, order = all_features(tokens, before, after)
    base, keyval = project(blocks, order, query_weight, key_value_weight)
    own_keyval = keyval.reshape(2, resp_dev, resp_len, kv_cols)
    mate_first = from_partner(own_keyval[:, 0], partner_xor_mask[0])
    got_down, shipped_up, mate_first, own_keyval = lax.optimization_barrier(
        (got_down, shipped_up, mate_first, own_keyval)
    )
    got_up = lax.all_to_all(shipped_up, "dp", split_axis=0, concat_axis=0, tiled=True)
    core = jnp.bitwise_and(lax.axis_index("tensor"), 1)
    keep, send = partial_rank_acts(
        tokens, got_down.reshape(-1, rank_extent, feature_shard), buffer_slot, core.reshape(1), rubrics
    )

    def split_sum(operands):
        keep, send, second = operands

        def beside(small):
            block, _ = lax.optimization_barrier((second, small))
            return from_partner(block, partner_xor_mask[1])

        return sum_over_tensor(keep, send, beside)

    def plain_sum(operands):
        keep, send, second = operands
        return sum_over_tensor_plain(keep, send, core, from_partner(second, partner_xor_mask[1]))

    same, other, mate_second = lax.cond(
        lengths[0] >= 1, split_sum, plain_sum, (keep, send, own_keyval[:, 1])
    )
    mate_keyval = jnp.concatenate([mate_first, mate_second], axis=1)
    own_lens = lax.dynamic_slice_in_dim(lengths, own_index * resp_dev, resp_dev)
    mate_index = partner_dev * resp_dev + jnp.arange(resp_dev, dtype=jnp.int32)
    mate_lens = jnp.take(lengths, mate_index, axis=0, mode="clip")
    mate_lens = jnp.where(partner_attend_mask == 1, mate_lens, 0)
    return attend(
        (same, other), base, keyval, mate_keyval, got_up.reshape(-1, rank_extent, head_columns),
        buffer_slot, own_lens, mate_lens, core.reshape(1), rubrics,
    )


def solution(mesh):
    in_specs = (
        P("dp", "tensor"),
        P(None, "tensor"),
        P(None, None, "tensor"),
        P("dp", None, "tensor"),
        P("dp", None, "tensor"),
        P("dp", None),
        P(),
        P("dp"),
        P(),
    )
    out_specs = P("dp", "tensor")
    return jax.shard_map(
        on_device, mesh=mesh, in_specs=in_specs, out_specs=out_specs, check_vma=False
    )
```

```python
from functools import partial
import math

import jax
import jax.numpy as jnp
from jax import lax
from jax.experimental import pallas as pl
from jax.experimental.pallas import tpu as pltpu
from jax.sharding import PartitionSpec as P

HEAD_SIZE = 128
MOST_PER_INDEX = 2
LANES = 128


def slot_layout(adapter_index, adapters_by_owner):
    owner_ids = adapter_index // adapters_by_owner
    local_ids = adapter_index % adapters_by_owner
    same_owner = owner_ids[:, None] == owner_ids[None, :]
    smaller = adapter_index[None, :] < adapter_index[:, None]
    owner_rank = jnp.any(same_owner & smaller, axis=1).astype(jnp.int32)
    return owner_ids, local_ids, owner_ids * MOST_PER_INDEX + owner_rank


def from_partner(block, mask):
    count = lax.axis_size("dp")
    moves = [
        partial(lax.ppermute, axis_name="dp", perm=[(source, source ^ flip) for source in range(count)])
        for flip in range(1, count)
    ]
    return lax.switch(mask - 1, moves, block)


def take_asked(table, asked):
    return jnp.take(table, asked[:, :MOST_PER_INDEX].reshape(-1), axis=0, mode="clip")


def project_kernel(pieces, carried, order_ref, query_weight_ref, keyval_weight_ref, *refs):
    sums, refs = refs[: 2 * carried], refs[2 * carried :]
    base_ref, keyval_ref, rows_ref, query_acc, keyval_acc, sems = refs[-6:]
    step = pl.program_id(0)
    last = len(pieces) - 1

    def fetches(i):
        copies, first = [], sum(pieces[:i])
        for piece in range(pieces[i]):
            source = refs[first + piece]
            rows = pl.ds(piece * source.shape[0], source.shape[0])
            copies.append(
                pltpu.make_async_copy(source, rows_ref.at[i % 2, rows], sems.at[i % 2, piece])
            )
        return copies

    @pl.when(step == 0)
    def _():
        for copy in fetches(0):
            copy.start()
        query_acc[...] = sums[0][...] if carried else jnp.zeros_like(query_acc)
        keyval_acc[...] = sums[1][...] if carried else jnp.zeros_like(keyval_acc)

    for i in range(len(pieces)):

        @pl.when(step == i)
        def _(i=i):
            if i < last:
                for copy in fetches(i + 1):
                    copy.start()
            for copy in fetches(i):
                copy.wait()

    rows = rows_ref[step % 2]
    both = jnp.concatenate([keyval_weight_ref[0], keyval_weight_ref[1]], axis=1)
    query_acc[...] += jnp.dot(rows, query_weight_ref[...], preferred_element_type=jnp.float32)
    keyval_acc[...] += jnp.dot(rows, both, preferred_element_type=jnp.float32)

    @pl.when(step == last)
    def _():
        base_ref[...] = query_acc[...]
        if carried:
            width = keyval_ref.shape[2]
            keyval_ref[0] = keyval_acc[:, :width].astype(keyval_ref.dtype)
            keyval_ref[1] = keyval_acc[:, width:].astype(keyval_ref.dtype)
        else:
            keyval_ref[...] = keyval_acc[...]


def project(blocks, order, query_weight, keyval_weight, sums=()):
    features = blocks[0][0].shape[1]
    rows = sum(piece.shape[0] for piece in blocks[0])
    pieces = tuple(len(block) for block in blocks)
    arrays = [piece for block in blocks for piece in block]
    columns = query_weight.shape[1]
    width = keyval_weight.shape[2]
    base = jax.ShapeDtypeStruct((rows, columns), jnp.float32)
    keyval_sums = jax.ShapeDtypeStruct((rows, 2 * width), jnp.float32)
    keyval = jax.ShapeDtypeStruct((2, rows, width), jnp.bfloat16) if sums else keyval_sums

    def whole(shape):
        return pl.BlockSpec(shape, lambda i, *_: (0,) * len(shape))

    return pl.pallas_call(
        partial(project_kernel, pieces, bool(sums)),
        out_shape=(pltpu.HBM(base.shape, base.dtype), pltpu.HBM(keyval.shape, keyval.dtype)),
        grid_spec=pltpu.PrefetchScalarGridSpec(
            num_scalar_prefetch=1,
            grid=(len(blocks),),
            in_specs=[
                pl.BlockSpec((features, columns), lambda i, order_ref: (order_ref[i], 0)),
                pl.BlockSpec((2, features, width), lambda i, order_ref: (0, order_ref[i], 0)),
            ]
            + [whole(x.shape) for x in sums]
            + [pl.BlockSpec(memory_space=pl.ANY)] * len(arrays),
            out_specs=(whole(base.shape), whole(keyval.shape)),
            scratch_shapes=[
                pltpu.VMEM((2, rows, features), jnp.bfloat16),
                pltpu.VMEM(base.shape, jnp.float32),
                pltpu.VMEM(keyval_sums.shape, jnp.float32),
                pltpu.SemaphoreType.DMA((2, max(pieces))),
            ],
        ),
        compiler_params=pltpu.CompilerParams(vmem_limit_bytes=32 << 20),
        cost_estimate=pl.CostEstimate(
            flops=2 * len(blocks) * rows * features * (columns + 2 * width),
            bytes_accessed=2 * len(blocks) * features * (rows + columns + 2 * width),
            transcendentals=0,
        ),
        name="project",
    )(
        order,
        *[pltpu.with_memory_space_constraint(x, pltpu.HBM) for x in (query_weight, keyval_weight)],
        *[pltpu.with_memory_space_constraint(x, pltpu.HBM) for x in sums],
        *arrays,
    )


def across_tensor(block, flip):
    size = lax.axis_size("tensor")
    return lax.ppermute(block, "tensor", [(source, source ^ flip) for source in range(size)])


def along_column(block, step):
    size = lax.axis_size("tensor")
    return lax.ppermute(block, "tensor", [(source, (source + 2 * step) % size) for source in range(size)])


def neighbour_features(tokens):
    return along_column(tokens, 1), along_column(tokens, -1)


def paired(held, offsets):
    size = lax.axis_size("tensor")
    own = lax.axis_index("tensor")
    blocks, order = [], []
    for offset, pieces in zip(offsets, held):
        index = (own + offset) % size
        blocks += [pieces, tuple(across_tensor(piece, 1) for piece in pieces)]
        order += [index, jnp.bitwise_xor(index, 1)]
    return blocks, jnp.stack(order)


def sum_over_tensor(keep, send, beside):
    size = lax.axis_size("tensor")
    pair = keep + across_tensor(send, 1)
    small = pair.astype(jnp.bfloat16)
    others = [across_tensor(small, flip) for flip in range(2, size, 2)]
    extra = beside(small)
    *others, extra = lax.optimization_barrier((*others, extra))
    total = pair
    for other in others:
        total = total + other.astype(jnp.float32)
    acts = total.astype(jnp.bfloat16)
    return acts, across_tensor(acts, 1), extra


def sum_over_tensor_plain(keep, send, core, extra):
    both = jnp.stack([keep, send])
    both = jnp.where(core == 0, both, both[::-1])
    total = both
    for flip in range(1, lax.axis_size("tensor")):
        total = total + across_tensor(both, flip)
    total = total.astype(jnp.bfloat16)
    total = jnp.where(core == 0, total, total[::-1])
    return total[0], total[1], extra


def partial_kernel(slots_ref, core_ref, tokens_ref, *refs):
    downs, keep_ref, send_ref = refs[:-2], refs[-2], refs[-1]
    rows = jnp.concatenate([d[0] for d in downs], axis=0)
    acts = lax.dot_general(
        tokens_ref[...], rows, (((1,), (1,)), ((), ())), preferred_element_type=jnp.float32
    )
    kept = pl.program_id(0) == core_ref[0]

    @pl.when(kept)
    def _():
        keep_ref[...] = acts

    @pl.when(jnp.logical_not(kept))
    def _():
        send_ref[...] = acts


def partial_rank_acts(tokens, got_down, slots, core, rubrics):
    rows, features = tokens.shape
    ranks = got_down.shape[1]
    resp_len = rows // 2

    def down_spec(s):
        return pl.BlockSpec((1, ranks, features), lambda j, slots_ref, _: (slots_ref[j * rubrics + s], 0, 0))

    half = jax.ShapeDtypeStruct((resp_len, rubrics * ranks), jnp.float32)
    half_spec = pl.BlockSpec(half.shape, lambda j, *_: (0, 0))
    return pl.pallas_call(
        partial_kernel,
        out_shape=(half, half),
        grid_spec=pltpu.PrefetchScalarGridSpec(
            num_scalar_prefetch=2,
            grid=(2,),
            in_specs=[pl.BlockSpec((resp_len, features), lambda j, *_: (j, 0))]
            + [down_spec(s) for s in range(rubrics)],
            out_specs=(half_spec, half_spec),
        ),
        compiler_params=pltpu.CompilerParams(vmem_limit_bytes=32 << 20),
        cost_estimate=pl.CostEstimate(flops=2 * rows * features * ranks * rubrics, bytes_accessed=4 << 20, transcendentals=0),
        name="partial_rank_acts",
    )(slots, core, tokens, *([got_down] * rubrics))


def attend_kernel(
    slots_ref, lens_ref, mates_ref, core_ref, same_ref, other_ref, base_ref, own_ref, *refs
):
    mate_refs, ups, out_ref = refs[:2], refs[2:-1], refs[-1]
    j = pl.program_id(0)
    mate = jnp.where(j == 0, mate_refs[0][...], mate_refs[1][...])
    acts = jnp.where(j == core_ref[0], same_ref[...], other_ref[...])
    up_rows = jnp.concatenate([u[0] for u in ups], axis=0)
    delta = jnp.dot(acts, up_rows, preferred_element_type=jnp.float32)
    queries = (base_ref[...] + delta).astype(jnp.bfloat16)
    rows, columns = queries.shape
    scale = math.log2(math.e) / math.sqrt(HEAD_SIZE)
    keys = jnp.concatenate([own_ref[0], mate[0]], axis=0)
    values = jnp.concatenate([own_ref[1], mate[1]], axis=0)
    position = lax.broadcasted_iota(jnp.int32, (rows, 2 * rows), 0)
    key_at = lax.broadcasted_iota(jnp.int32, (rows, 2 * rows), 1)
    own_ok = (key_at <= position) & (key_at < lens_ref[j])
    mate_ok = (key_at >= rows) & (key_at < rows + mates_ref[j])
    allowed = own_ok | mate_ok
    for h in range(columns // HEAD_SIZE):
        cut = slice(h * HEAD_SIZE, (h + 1) * HEAD_SIZE)
        scores = lax.dot_general(
            queries[:, cut], keys, (((1,), (1,)), ((), ())), preferred_element_type=jnp.float32
        )
        scores = jnp.where(allowed, scores, -1e30)
        top = jnp.max(scores, axis=1, keepdims=True)
        raised = jnp.exp2((scores - top) * scale)
        weights = (raised * (1.0 / jnp.sum(raised, axis=1, keepdims=True))).astype(jnp.bfloat16)
        out_ref[:, cut] = jnp.dot(weights, values, preferred_element_type=jnp.float32).astype(
            out_ref.dtype
        )


def attend(acts, base, keyval, mate_keyvals, got_up, slots, own_lens, mate_lens, core, rubrics):
    rows, columns = base.shape
    resp_dev = own_lens.shape[0]
    resp_len = rows // resp_dev
    ranks = got_up.shape[1]

    def up_spec(s):
        return pl.BlockSpec((1, ranks, columns), lambda j, slots_ref, *_: (slots_ref[j * rubrics + s], 0, 0))

    acts_spec = pl.BlockSpec(acts[0].shape, lambda j, *_: (0, 0))
    mate_spec = pl.BlockSpec((2, resp_len, HEAD_SIZE), lambda j, *_: (0, 0, 0))
    return pl.pallas_call(
        attend_kernel,
        out_shape=jax.ShapeDtypeStruct((rows, columns), jnp.bfloat16),
        grid_spec=pltpu.PrefetchScalarGridSpec(
            num_scalar_prefetch=4,
            grid=(resp_dev,),
            in_specs=[
                acts_spec,
                acts_spec,
                pl.BlockSpec((resp_len, columns), lambda j, *_: (j, 0)),
                pl.BlockSpec((2, resp_len, HEAD_SIZE), lambda j, *_: (0, j, 0)),
                mate_spec,
                mate_spec,
            ]
            + [up_spec(s) for s in range(rubrics)],
            out_specs=pl.BlockSpec((resp_len, columns), lambda j, *_: (j, 0)),
        ),
        compiler_params=pltpu.CompilerParams(vmem_limit_bytes=40 << 20),
        name="attend",
    )(slots, own_lens, mate_lens, core, *acts, pltpu.with_memory_space_constraint(base, pltpu.HBM), keyval, *mate_keyvals, *([got_up] * rubrics))


def on_device(
    tokens,
    query_weight,
    key_value_weight,
    adapter_down_weight,
    adapter_up_weight,
    response_rubrics,
    lengths,
    partner_attend_mask,
    partner_xor_mask,
):
    owner_groups = lax.axis_size("dp")
    own_index = lax.axis_index("dp")
    resp_dev, rubrics = response_rubrics.shape
    partner_dev = jnp.bitwise_xor(own_index, partner_xor_mask)
    adapters_by_owner, rank_extent, feature_shard = adapter_down_weight.shape
    head_columns = query_weight.shape[1]
    kv_cols = key_value_weight.shape[2]
    slot_count = resp_dev * rubrics
    tok_rows = tokens.shape[0]
    resp_len = tok_rows // resp_dev
    before, after = neighbour_features(tokens)
    slot_ids = response_rubrics.reshape(slot_count)
    owner_ids, local_ids, buffer_slot = slot_layout(slot_ids, adapters_by_owner)
    cells = lax.broadcasted_iota(jnp.int32, (owner_groups, LANES), 0) * MOST_PER_INDEX
    lane = lax.broadcasted_iota(jnp.int32, (owner_groups, LANES), 1)
    cells = jnp.where(lane < MOST_PER_INDEX, cells + lane, -1)
    wanted = jnp.max(
        jnp.where(buffer_slot[:, None, None] == cells[None], local_ids[:, None, None], 0), axis=0
    )
    asked = lax.all_to_all(wanted, "dp", split_axis=0, concat_axis=0, tiled=True)
    shipped_down = take_asked(adapter_down_weight, asked)
    shipped_down = shipped_down.reshape(owner_groups, MOST_PER_INDEX, rank_extent, feature_shard)
    got_down = lax.all_to_all(shipped_down, "dp", split_axis=0, concat_axis=0, tiled=True)
    shipped_up = take_asked(adapter_up_weight, asked)
    shipped_up = shipped_up.reshape(owner_groups, MOST_PER_INDEX, rank_extent, head_columns)
    before, after, shipped_up = lax.optimization_barrier((before, after, shipped_up))
    half = tok_rows // 2
    opposite = (along_column(before[:half], 1), along_column(after[half:], -1))
    near, order = paired([(tokens,), (before,), (after,)], (0, -2, 2))
    sums = project(near, order, query_weight, key_value_weight)
    opposite, sums = lax.optimization_barrier((opposite, sums))
    far, order = paired([opposite], (4,))
    base, keyval = project(far, order, query_weight, key_value_weight, sums)
    own_keyval = keyval.reshape(2, resp_dev, resp_len, kv_cols)
    mate_first = from_partner(own_keyval[:, 0], partner_xor_mask[0])
    got_down, shipped_up, mate_first, own_keyval = lax.optimization_barrier(
        (got_down, shipped_up, mate_first, own_keyval)
    )
    got_up = lax.all_to_all(shipped_up, "dp", split_axis=0, concat_axis=0, tiled=True)
    core = jnp.bitwise_and(lax.axis_index("tensor"), 1)
    keep, send = partial_rank_acts(
        tokens, got_down.reshape(-1, rank_extent, feature_shard), buffer_slot, core.reshape(1), rubrics
    )

    def split_sum(operands):
        keep, send, second = operands

        def beside(small):
            block, _ = lax.optimization_barrier((second, small))
            return from_partner(block, partner_xor_mask[1])

        return sum_over_tensor(keep, send, beside)

    def plain_sum(operands):
        keep, send, second = operands
        return sum_over_tensor_plain(keep, send, core, from_partner(second, partner_xor_mask[1]))

    same, other, mate_second = lax.cond(
        lengths[0] >= 1, split_sum, plain_sum, (keep, send, own_keyval[:, 1])
    )
    own_lens = lax.dynamic_slice_in_dim(lengths, own_index * resp_dev, resp_dev)
    mate_index = partner_dev * resp_dev + jnp.arange(resp_dev, dtype=jnp.int32)
    mate_lens = jnp.take(lengths, mate_index, axis=0, mode="clip")
    mate_lens = jnp.where(partner_attend_mask == 1, mate_lens, 0)
    return attend(
        (same, other), base, keyval, (mate_first, mate_second), got_up.reshape(-1, rank_extent, head_columns),
        buffer_slot, own_lens, mate_lens, core.reshape(1), rubrics,
    )


def solution(mesh):
    in_specs = (
        P("dp", "tensor"),
        P(None, "tensor"),
        P(None, None, "tensor"),
        P("dp", None, "tensor"),
        P("dp", None, "tensor"),
        P("dp", None),
        P(),
        P("dp"),
        P(),
    )
    out_specs = P("dp", "tensor")
    return jax.shard_map(
        on_device, mesh=mesh, in_specs=in_specs, out_specs=out_specs, check_vma=False
    )
```

```python
from functools import partial
import math

import jax
import jax.numpy as jnp
from jax import lax
from jax.experimental import pallas as pl
from jax.experimental.pallas import tpu as pltpu
from jax.sharding import PartitionSpec as P

HEAD_SIZE = 128
MOST_PER_INDEX = 2
LANES = 128


def slot_layout(adapter_index, adapters_by_owner):
    owner_ids = adapter_index // adapters_by_owner
    local_ids = adapter_index % adapters_by_owner
    same_owner = owner_ids[:, None] == owner_ids[None, :]
    smaller = adapter_index[None, :] < adapter_index[:, None]
    owner_rank = jnp.any(same_owner & smaller, axis=1).astype(jnp.int32)
    return owner_ids, local_ids, owner_ids * MOST_PER_INDEX + owner_rank


def from_partner(block, mask):
    count = lax.axis_size("dp")
    moves = [
        partial(lax.ppermute, axis_name="dp", perm=[(source, source ^ flip) for source in range(count)])
        for flip in range(1, count)
    ]
    return lax.switch(mask - 1, moves, block)


def take_kernel(asked_ref, table_ref, out_ref, rows_ref, in_sems, out_sems):
    count = out_ref.shape[0]

    def fetch(i):
        index = asked_ref[i // MOST_PER_INDEX, i % MOST_PER_INDEX]
        return pltpu.make_async_copy(table_ref.at[jnp.maximum(index, 0)], rows_ref.at[i], in_sems.at[i])

    def store(i):
        return pltpu.make_async_copy(rows_ref.at[i], out_ref.at[i], out_sems.at[i])

    def for_asked(step):
        for i in range(count):

            @pl.when(asked_ref[i // MOST_PER_INDEX, i % MOST_PER_INDEX] >= 0)
            def _(i=i):
                step(i)

    def pass_on(i):
        fetch(i).wait()
        store(i).start()

    for_asked(lambda i: fetch(i).start())
    for_asked(pass_on)
    for_asked(lambda i: store(i).wait())


def take_asked(table, asked):
    count = asked.shape[0] * MOST_PER_INDEX
    shape = (count,) + table.shape[1:]
    return pl.pallas_call(
        take_kernel,
        out_shape=jax.ShapeDtypeStruct(shape, table.dtype),
        grid_spec=pltpu.PrefetchScalarGridSpec(
            num_scalar_prefetch=1,
            grid=(1,),
            in_specs=[pl.BlockSpec(memory_space=pl.ANY)],
            out_specs=pl.BlockSpec(memory_space=pl.ANY),
            scratch_shapes=[
                pltpu.VMEM(shape, table.dtype),
                pltpu.SemaphoreType.DMA((count,)),
                pltpu.SemaphoreType.DMA((count,)),
            ],
        ),
        name="take_asked",
    )(asked, table)


def project_kernel(pieces, carried, order_ref, query_weight_ref, keyval_weight_ref, *refs):
    sums, refs = refs[: 2 * carried], refs[2 * carried :]
    base_ref, keyval_ref, rows_ref, query_acc, keyval_acc, sems = refs[-6:]
    step = pl.program_id(0)
    last = len(pieces) - 1

    def fetches(i):
        copies, first = [], sum(pieces[:i])
        for piece in range(pieces[i]):
            source = refs[first + piece]
            rows = pl.ds(piece * source.shape[0], source.shape[0])
            copies.append(
                pltpu.make_async_copy(source, rows_ref.at[i % 2, rows], sems.at[i % 2, piece])
            )
        return copies

    @pl.when(step == 0)
    def _():
        for copy in fetches(0):
            copy.start()
        query_acc[...] = sums[0][...] if carried else jnp.zeros_like(query_acc)
        keyval_acc[...] = sums[1][...] if carried else jnp.zeros_like(keyval_acc)

    for i in range(len(pieces)):

        @pl.when(step == i)
        def _(i=i):
            if i < last:
                for copy in fetches(i + 1):
                    copy.start()
            for copy in fetches(i):
                copy.wait()

    rows = rows_ref[step % 2]
    both = jnp.concatenate([keyval_weight_ref[0], keyval_weight_ref[1]], axis=1)
    query_acc[...] += jnp.dot(rows, query_weight_ref[...], preferred_element_type=jnp.float32)
    keyval_acc[...] += jnp.dot(rows, both, preferred_element_type=jnp.float32)

    @pl.when(step == last)
    def _():
        base_ref[...] = query_acc[...]
        if carried:
            width = keyval_ref.shape[2]
            keyval_ref[0] = keyval_acc[:, :width].astype(keyval_ref.dtype)
            keyval_ref[1] = keyval_acc[:, width:].astype(keyval_ref.dtype)
        else:
            keyval_ref[...] = keyval_acc[...]


def project(blocks, order, query_weight, keyval_weight, sums=()):
    features = blocks[0][0].shape[1]
    rows = sum(piece.shape[0] for piece in blocks[0])
    pieces = tuple(len(block) for block in blocks)
    arrays = [piece for block in blocks for piece in block]
    columns = query_weight.shape[1]
    width = keyval_weight.shape[2]
    base = jax.ShapeDtypeStruct((rows, columns), jnp.float32)
    keyval_sums = jax.ShapeDtypeStruct((rows, 2 * width), jnp.float32)
    keyval = jax.ShapeDtypeStruct((2, rows, width), jnp.bfloat16) if sums else keyval_sums

    def whole(shape):
        return pl.BlockSpec(shape, lambda i, *_: (0,) * len(shape))

    return pl.pallas_call(
        partial(project_kernel, pieces, bool(sums)),
        out_shape=(pltpu.HBM(base.shape, base.dtype), pltpu.HBM(keyval.shape, keyval.dtype)),
        grid_spec=pltpu.PrefetchScalarGridSpec(
            num_scalar_prefetch=1,
            grid=(len(blocks),),
            in_specs=[
                pl.BlockSpec((features, columns), lambda i, order_ref: (order_ref[i], 0)),
                pl.BlockSpec((2, features, width), lambda i, order_ref: (0, order_ref[i], 0)),
            ]
            + [whole(x.shape) for x in sums]
            + [pl.BlockSpec(memory_space=pl.ANY)] * len(arrays),
            out_specs=(whole(base.shape), whole(keyval.shape)),
            scratch_shapes=[
                pltpu.VMEM((2, rows, features), jnp.bfloat16),
                pltpu.VMEM(base.shape, jnp.float32),
                pltpu.VMEM(keyval_sums.shape, jnp.float32),
                pltpu.SemaphoreType.DMA((2, max(pieces))),
            ],
        ),
        compiler_params=pltpu.CompilerParams(vmem_limit_bytes=32 << 20),
        cost_estimate=pl.CostEstimate(
            flops=2 * len(blocks) * rows * features * (columns + 2 * width),
            bytes_accessed=2 * len(blocks) * features * (rows + columns + 2 * width),
            transcendentals=0,
        ),
        name="project",
    )(
        order,
        *[pltpu.with_memory_space_constraint(x, pltpu.HBM) for x in (query_weight, keyval_weight)],
        *[pltpu.with_memory_space_constraint(x, pltpu.HBM) for x in sums],
        *arrays,
    )


def across_tensor(block, flip):
    size = lax.axis_size("tensor")
    return lax.ppermute(block, "tensor", [(source, source ^ flip) for source in range(size)])


def along_column(block, step):
    size = lax.axis_size("tensor")
    return lax.ppermute(block, "tensor", [(source, (source + 2 * step) % size) for source in range(size)])


def neighbour_features(tokens):
    return along_column(tokens, 1), along_column(tokens, -1)


def paired(held, offsets):
    size = lax.axis_size("tensor")
    own = lax.axis_index("tensor")
    blocks, order = [], []
    for offset, pieces in zip(offsets, held):
        index = (own + offset) % size
        blocks += [pieces, tuple(across_tensor(piece, 1) for piece in pieces)]
        order += [index, jnp.bitwise_xor(index, 1)]
    return blocks, jnp.stack(order)


def sum_over_tensor(keep, send, beside):
    size = lax.axis_size("tensor")
    pair = keep + across_tensor(send, 1)
    small = pair.astype(jnp.bfloat16)
    others = [across_tensor(small, flip) for flip in range(2, size, 2)]
    extra = beside(small)
    *others, extra = lax.optimization_barrier((*others, extra))
    total = pair
    for other in others:
        total = total + other.astype(jnp.float32)
    acts = total.astype(jnp.bfloat16)
    return acts, across_tensor(acts, 1), extra


def sum_over_tensor_plain(keep, send, core, extra):
    both = jnp.stack([keep, send])
    both = jnp.where(core == 0, both, both[::-1])
    total = both
    for flip in range(1, lax.axis_size("tensor")):
        total = total + across_tensor(both, flip)
    total = total.astype(jnp.bfloat16)
    total = jnp.where(core == 0, total, total[::-1])
    return total[0], total[1], extra


def block_copies(slots_ref, source_ref, rows_ref, sems, rubrics, first, count):
    ranks = source_ref.shape[1]
    return [
        pltpu.make_async_copy(
            source_ref.at[slots_ref[j * rubrics + s]],
            rows_ref.at[j, pl.ds(s * ranks, ranks)],
            sems.at[j * rubrics + s],
        )
        for j in range(first, first + count)
        for s in range(rubrics)
    ]


def partial_kernel(rubrics, slots_ref, core_ref, tokens_ref, down_ref, keep_ref, send_ref, rows_ref, sems):
    copies = block_copies(slots_ref, down_ref, rows_ref, sems, rubrics, 0, 2)
    for copy in copies:
        copy.start()
    for copy in copies:
        copy.wait()
    resp_len = keep_ref.shape[0]
    for out_ref, j in ((send_ref, 1 - core_ref[0]), (keep_ref, core_ref[0])):
        out_ref[...] = lax.dot_general(
            tokens_ref[pl.ds(j * resp_len, resp_len), :], rows_ref[j], (((1,), (1,)), ((), ())),
            preferred_element_type=jnp.float32,
        )


def partial_rank_acts(tokens, got_down, slots, core, rubrics):
    rows, features = tokens.shape
    ranks = got_down.shape[1]
    half = jax.ShapeDtypeStruct((rows // 2, rubrics * ranks), jnp.float32)
    half_spec = pl.BlockSpec(half.shape, lambda i, *_: (0, 0))
    return pl.pallas_call(
        partial(partial_kernel, rubrics),
        out_shape=(half, half),
        grid_spec=pltpu.PrefetchScalarGridSpec(
            num_scalar_prefetch=2,
            grid=(1,),
            in_specs=[
                pl.BlockSpec((rows, features), lambda i, *_: (0, 0)),
                pl.BlockSpec(memory_space=pl.ANY),
            ],
            out_specs=(half_spec, half_spec),
            scratch_shapes=[
                pltpu.VMEM((2, rubrics * ranks, features), jnp.bfloat16),
                pltpu.SemaphoreType.DMA((2 * rubrics,)),
            ],
        ),
        compiler_params=pltpu.CompilerParams(vmem_limit_bytes=32 << 20),
        name="partial_rank_acts",
    )(slots, core, tokens, got_down)


def attend_kernel(
    slots_ref, lens_ref, mates_ref, core_ref, same_ref, other_ref, base_ref, own_ref, *refs
):
    mate_refs, ups, out_ref = refs[:2], refs[2:-1], refs[-1]
    j = pl.program_id(0)
    mate = jnp.where(j == 0, mate_refs[0][...], mate_refs[1][...])
    acts = jnp.where(j == core_ref[0], same_ref[...], other_ref[...])
    up_rows = jnp.concatenate([u[0] for u in ups], axis=0)
    delta = jnp.dot(acts, up_rows, preferred_element_type=jnp.float32)
    queries = (base_ref[...] + delta).astype(jnp.bfloat16)
    rows, columns = queries.shape
    scale = math.log2(math.e) / math.sqrt(HEAD_SIZE)
    keys = jnp.concatenate([own_ref[0], mate[0]], axis=0)
    values = jnp.concatenate([own_ref[1], mate[1]], axis=0)
    position = lax.broadcasted_iota(jnp.int32, (rows, 2 * rows), 0)
    key_at = lax.broadcasted_iota(jnp.int32, (rows, 2 * rows), 1)
    own_ok = (key_at <= position) & (key_at < lens_ref[j])
    mate_ok = (key_at >= rows) & (key_at < rows + mates_ref[j])
    allowed = own_ok | mate_ok
    for h in range(columns // HEAD_SIZE):
        cut = slice(h * HEAD_SIZE, (h + 1) * HEAD_SIZE)
        scores = lax.dot_general(
            queries[:, cut], keys, (((1,), (1,)), ((), ())), preferred_element_type=jnp.float32
        )
        scores = jnp.where(allowed, scores, -1e30)
        top = jnp.max(scores, axis=1, keepdims=True)
        raised = jnp.exp2((scores - top) * scale)
        weights = (raised * (1.0 / jnp.sum(raised, axis=1, keepdims=True))).astype(jnp.bfloat16)
        out_ref[:, cut] = jnp.dot(weights, values, preferred_element_type=jnp.float32).astype(
            out_ref.dtype
        )


def attend(acts, base, keyval, mate_keyvals, got_up, slots, own_lens, mate_lens, core, rubrics):
    rows, columns = base.shape
    resp_dev = own_lens.shape[0]
    resp_len = rows // resp_dev
    ranks = got_up.shape[1]

    def up_spec(s):
        return pl.BlockSpec((1, ranks, columns), lambda j, slots_ref, *_: (slots_ref[j * rubrics + s], 0, 0))

    acts_spec = pl.BlockSpec(acts[0].shape, lambda j, *_: (0, 0))
    mate_spec = pl.BlockSpec((2, resp_len, HEAD_SIZE), lambda j, *_: (0, 0, 0))
    return pl.pallas_call(
        attend_kernel,
        out_shape=jax.ShapeDtypeStruct((rows, columns), jnp.bfloat16),
        grid_spec=pltpu.PrefetchScalarGridSpec(
            num_scalar_prefetch=4,
            grid=(resp_dev,),
            in_specs=[
                acts_spec,
                acts_spec,
                pl.BlockSpec((resp_len, columns), lambda j, *_: (j, 0)),
                pl.BlockSpec((2, resp_len, HEAD_SIZE), lambda j, *_: (0, j, 0)),
                mate_spec,
                mate_spec,
            ]
            + [up_spec(s) for s in range(rubrics)],
            out_specs=pl.BlockSpec((resp_len, columns), lambda j, *_: (j, 0)),
        ),
        compiler_params=pltpu.CompilerParams(vmem_limit_bytes=40 << 20),
        name="attend",
    )(slots, own_lens, mate_lens, core, *acts, pltpu.with_memory_space_constraint(base, pltpu.HBM), keyval, *mate_keyvals, *([got_up] * rubrics))


def on_device(
    tokens,
    query_weight,
    key_value_weight,
    adapter_down_weight,
    adapter_up_weight,
    response_rubrics,
    lengths,
    partner_attend_mask,
    partner_xor_mask,
):
    owner_groups = lax.axis_size("dp")
    own_index = lax.axis_index("dp")
    resp_dev, rubrics = response_rubrics.shape
    partner_dev = jnp.bitwise_xor(own_index, partner_xor_mask)
    adapters_by_owner, rank_extent, feature_shard = adapter_down_weight.shape
    head_columns = query_weight.shape[1]
    kv_cols = key_value_weight.shape[2]
    slot_count = resp_dev * rubrics
    tok_rows = tokens.shape[0]
    resp_len = tok_rows // resp_dev
    before, after = neighbour_features(tokens)
    slot_ids = response_rubrics.reshape(slot_count)
    owner_ids, local_ids, buffer_slot = slot_layout(slot_ids, adapters_by_owner)
    cells = lax.broadcasted_iota(jnp.int32, (owner_groups, LANES), 0) * MOST_PER_INDEX
    lane = lax.broadcasted_iota(jnp.int32, (owner_groups, LANES), 1)
    cells = jnp.where(lane < MOST_PER_INDEX, cells + lane, -1)
    wanted = jnp.max(
        jnp.where(buffer_slot[:, None, None] == cells[None], local_ids[:, None, None], -1), axis=0
    )
    asked = lax.all_to_all(wanted, "dp", split_axis=0, concat_axis=0, tiled=True)
    shipped_down = take_asked(adapter_down_weight, asked)
    shipped_down = shipped_down.reshape(owner_groups, MOST_PER_INDEX, rank_extent, feature_shard)
    got_down = lax.all_to_all(shipped_down, "dp", split_axis=0, concat_axis=0, tiled=True)
    shipped_up = take_asked(adapter_up_weight, asked)
    shipped_up = shipped_up.reshape(owner_groups, MOST_PER_INDEX, rank_extent, head_columns)
    own_lens = lax.dynamic_slice_in_dim(lengths, own_index * resp_dev, resp_dev)
    mate_index = partner_dev * resp_dev + jnp.arange(resp_dev, dtype=jnp.int32)
    mate_lens = jnp.take(lengths, mate_index, axis=0, mode="clip")
    mate_lens = jnp.where(partner_attend_mask == 1, mate_lens, 0)
    before, after, shipped_up, own_lens, mate_lens = lax.optimization_barrier(
        (before, after, shipped_up, own_lens, mate_lens)
    )
    half = tok_rows // 2
    opposite = (along_column(before[:half], 1), along_column(after[half:], -1))
    near, order = paired([(tokens,), (before,), (after,)], (0, -2, 2))
    sums = project(near, order, query_weight, key_value_weight)
    opposite, sums = lax.optimization_barrier((opposite, sums))
    far, order = paired([opposite], (4,))
    base, keyval = project(far, order, query_weight, key_value_weight, sums)
    own_keyval = keyval.reshape(2, resp_dev, resp_len, kv_cols)
    mate_first = from_partner(own_keyval[:, 0], partner_xor_mask[0])
    got_down, shipped_up, mate_first, own_keyval = lax.optimization_barrier(
        (got_down, shipped_up, mate_first, own_keyval)
    )
    got_up = lax.all_to_all(shipped_up, "dp", split_axis=0, concat_axis=0, tiled=True)
    core = jnp.bitwise_and(lax.axis_index("tensor"), 1)
    keep, send = partial_rank_acts(
        tokens, got_down.reshape(-1, rank_extent, feature_shard), buffer_slot, core.reshape(1), rubrics
    )

    def split_sum(operands):
        keep, send, second = operands

        def beside(small):
            block, _ = lax.optimization_barrier((second, small))
            return from_partner(block, partner_xor_mask[1])

        return sum_over_tensor(keep, send, beside)

    def plain_sum(operands):
        keep, send, second = operands
        return sum_over_tensor_plain(keep, send, core, from_partner(second, partner_xor_mask[1]))

    same, other, mate_second = lax.cond(
        lengths[0] >= 1, split_sum, plain_sum, (keep, send, own_keyval[:, 1])
    )
    return attend(
        (same, other), base, keyval, (mate_first, mate_second), got_up.reshape(-1, rank_extent, head_columns),
        buffer_slot, own_lens, mate_lens, core.reshape(1), rubrics,
    )


def solution(mesh):
    in_specs = (
        P("dp", "tensor"),
        P(None, "tensor"),
        P(None, None, "tensor"),
        P("dp", None, "tensor"),
        P("dp", None, "tensor"),
        P("dp", None),
        P(),
        P("dp"),
        P(),
    )
    out_specs = P("dp", "tensor")
    return jax.shard_map(
        on_device, mesh=mesh, in_specs=in_specs, out_specs=out_specs, check_vma=False
    )
```
